32 devices in a mesh: snap: 4 (over z), cell: 8 (over y, x, core).
Axes of the slice: x: 2, y: 2, z: 4, core: 2. Of those that a mesh axis runs over, the one named last changes fastest.
Arguments:
- pressure: float32 [8320, 16384], P('snap', 'cell'), may hold values from -180 to 180
- block_starts: int32 [64], replicated, may hold values from 0 to 8064, as said below
- retained_bins: int32 [64], replicated, may hold values from 0 to 127
Outputs:
- spectral_gram: float32 [64, 2, 64, 64], P('snap')
The draws below stay inside these ranges and needn't reach their ends.
Inputs may be any that keep to these rules, and one draw needn't show every extreme that they name: `block_starts`: the 64 values are distinct multiples of 128.
All inputs are finite; a program needn't handle non-finite values.
Results may differ from the reference program's by a relative error of at most 0.0003.
Values sent between devices are 32-bit elements; how exact they have to be, the bound alone decides.
A program may use at most 128 MiB of HBM per device.

```python
import jax
import jax.numpy as jnp
from jax import lax

NFFT = 256
HOP = 128
BLOCKS = 64
SNAPS = 8320
K = 64
CELL_DEV = 2048
CELLS = 16384


def draw_pressure(key, part):
    subkeys = jax.random.split(key, 3)
    cells = jnp.arange(CELLS, dtype=jnp.float32)
    cell_scale = jnp.exp(jnp.log(10.0) * cells / CELLS) * jax.random.uniform(subkeys[1], (CELLS,), minval=0.7, maxval=1.4)
    time_scale = jnp.exp(jax.random.uniform(subkeys[2], (SNAPS, 1), minval=jnp.log(0.4), maxval=jnp.log(2.5)))
    values = jax.random.truncated_normal(subkeys[0], -5.0, 5.0, (SNAPS, CELLS))
    return (values * time_scale * cell_scale[None, :]).astype(jnp.float32)


def draw_block_starts(key, part):
    order = jax.random.permutation(jax.random.fold_in(key, 17), BLOCKS)
    return (order * HOP).astype(jnp.int32)


def place_ends(drawn, stream_key, low, top_value):
    longest = drawn.shape.index(max(drawn.shape))
    spots = []
    for shift in (0, 1):
        where = [jax.random.randint(jax.random.fold_in(stream_key, axis), (), 0, length) for axis, length in enumerate(drawn.shape)]
        where[longest] = (where[longest] + shift) % drawn.shape[longest]
        spots.append(tuple(where))
    return drawn.at[spots[0]].set(low).at[spots[1]].set(top_value)


def setup_inputs(seed: int = 0) -> dict:
    splits = jax.random.split(jax.random.key(seed), 4)
    return {
        "pressure": draw_pressure(jax.random.fold_in(splits[3], 71), 0),
        "block_starts": draw_block_starts(jax.random.fold_in(splits[3], 71), 0),
        "retained_bins": place_ends(jax.random.randint(splits[2], (K,), 0, HOP), jax.random.fold_in(splits[2], 1), 0, HOP - 1).astype(jnp.int32),
    }


def make_table(retained_bins):
    offsets = jnp.arange(NFFT, dtype=jnp.int32)
    window = 0.5 - 0.5 * jnp.cos(2.0 * jnp.pi * offsets.astype(jnp.float32) / NFFT)
    norm_factor = 1.0 / jnp.sqrt(jnp.sum(window * window))
    phase_steps = retained_bins[:, None] * offsets[None, :] % NFFT
    angles = 2.0 * jnp.pi * phase_steps.astype(jnp.float32) / NFFT
    wave_table = jnp.stack([window * norm_factor * jnp.cos(angles), -window * norm_factor * jnp.sin(angles)], 1)
    return wave_table.reshape(2 * retained_bins.shape[0], NFFT)

def reference(pressure, block_starts, retained_bins):
    wave_table = make_table(retained_bins)
    block_count = CELLS // CELL_DEV

    def accumulate(total_gram, block_number):
        column_block = lax.dynamic_slice_in_dim(pressure, (block_number * CELL_DEV).astype(jnp.int32), CELL_DEV, 1)
        windows = jax.vmap(lambda anchor: lax.dynamic_slice_in_dim(column_block, anchor.astype(jnp.int32), NFFT, 0))(block_starts)
        spectra = jnp.einsum('rt,btc->rbc', wave_table, windows, precision=lax.Precision.HIGHEST)
        stacked = spectra.reshape(K, 2 * BLOCKS, CELL_DEV)
        products = jnp.einsum('kbc,kdc->kbd', stacked, stacked, precision=lax.Precision.HIGHEST)
        return (total_gram + products, None)
    initial = jnp.zeros((K, 2 * BLOCKS, 2 * BLOCKS), jnp.float32)
    total_gram, unused = lax.scan(accumulate, initial, jnp.arange(block_count, dtype=jnp.int32))
    real_part = total_gram[:, :BLOCKS, :BLOCKS] + total_gram[:, BLOCKS:, BLOCKS:]
    imag_part = total_gram[:, :BLOCKS, BLOCKS:] - total_gram[:, BLOCKS:, :BLOCKS]
    return jnp.stack([real_part, imag_part], 1) / CELLS
```

```python
import jax
import jax.numpy as jnp
from jax import lax
from jax.sharding import PartitionSpec as P

NFFT = 256
LANES = 128
MAX_CHUNKS = 4


def make_table(retained_bins):
    offsets = jnp.arange(NFFT, dtype=jnp.int32)
    window = 0.5 - 0.5 * jnp.cos(2.0 * jnp.pi * offsets.astype(jnp.float32) / NFFT)
    norm_factor = 1.0 / jnp.sqrt(jnp.sum(window * window))
    phase_steps = retained_bins[:, None] * offsets[None, :] % NFFT
    angles = 2.0 * jnp.pi * phase_steps.astype(jnp.float32) / NFFT
    wave_table = jnp.stack(
        [window * norm_factor * jnp.cos(angles), -window * norm_factor * jnp.sin(angles)], 1
    )
    return wave_table.reshape(2 * retained_bins.shape[0], NFFT)


def chunk_products(series, wave_table, kept_count, blocks):
    half_len = NFFT // 2
    segments = series.reshape(series.shape[0] // half_len, half_len, series.shape[1])
    front = jnp.einsum("rt,stc->rsc", wave_table[:, :half_len], segments[:-1], precision=lax.Precision.HIGHEST)
    back = jnp.einsum("rt,stc->rsc", wave_table[:, half_len:], segments[1:], precision=lax.Precision.HIGHEST)
    stacked = (front + back).reshape(kept_count, 2 * blocks, series.shape[1])
    return jnp.einsum("kbc,kdc->kbd", stacked, stacked, precision=lax.Precision.HIGHEST)


def on_device(pressure, block_starts, retained_bins):
    snap_count = lax.axis_size("snap")
    row_count, width_local = pressure.shape
    pieces = width_local // snap_count
    chunks = max(n for n in range(1, MAX_CHUNKS + 1) if pieces % (n * LANES) == 0)
    wide = pieces // chunks
    wave_table = make_table(retained_bins)
    kept_count = retained_bins.shape[0]
    blocks = block_starts.shape[0]
    received = []
    for i in range(chunks):
        columns = pressure[:, i * snap_count * wide:(i + 1) * snap_count * wide]
        shaped = columns.reshape(row_count, snap_count, wide)
        received.append(lax.all_to_all(shaped, "snap", split_axis=1, concat_axis=0, tiled=True)[:, 0, :])
    products = chunk_products(received[0], wave_table, kept_count, blocks)
    for series in received[1:]:
        products = products + chunk_products(series, wave_table, kept_count, blocks)
    real_part = products[:, :blocks, :blocks] + products[:, blocks:, blocks:]
    imag_part = products[:, :blocks, blocks:] - products[:, blocks:, :blocks]
    local_gram = jnp.stack([real_part, imag_part], 1)
    cell_total = width_local * lax.axis_size("cell")
    partial_gram = lax.psum_scatter(local_gram, "snap", scatter_dimension=0, tiled=True)
    own_block = lax.psum(partial_gram, "cell") / cell_total
    order = (block_starts[:, None] // (NFFT // 2) == jnp.arange(blocks)[None, :]).astype(jnp.float32)
    turned = jnp.einsum("kpij,dj->kpid", own_block, order, precision=lax.Precision.HIGHEST)
    return jnp.einsum("bi,kpid->kpbd", order, turned, precision=lax.Precision.HIGHEST)


def solution(mesh):
    placed = (P("snap", "cell"), P(), P())
    return jax.shard_map(
        on_device,
        mesh=mesh,
        in_specs=placed,
        out_specs=P("snap", None, None, None),
        check_vma=False,
    )
```

```python
import functools

import jax
import jax.numpy as jnp
from jax import lax
from jax.experimental import pallas as pl
from jax.experimental.pallas import tpu as pltpu
from jax.sharding import PartitionSpec as P

NFFT = 256
LANES = 128
MAX_CHUNKS = 4
MESH = pl.DeviceIdType.MESH


def make_table(retained_bins):
    offsets = jnp.arange(NFFT, dtype=jnp.int32)
    window = 0.5 - 0.5 * jnp.cos(2.0 * jnp.pi * offsets.astype(jnp.float32) / NFFT)
    norm_factor = 1.0 / jnp.sqrt(jnp.sum(window * window))
    phase_steps = retained_bins[:, None] * offsets[None, :] % NFFT
    angles = 2.0 * jnp.pi * phase_steps.astype(jnp.float32) / NFFT
    wave_table = jnp.stack(
        [window * norm_factor * jnp.cos(angles), -window * norm_factor * jnp.sin(angles)], 1
    )
    return wave_table.reshape(2 * retained_bins.shape[0], NFFT)


def chunk_products(series, wave_table, kept_count, blocks):
    half_len = NFFT // 2
    segments = series.reshape(series.shape[0] // half_len, half_len, series.shape[1])
    front = jnp.einsum("rt,stc->rsc", wave_table[:, :half_len], segments[:-1], precision=lax.Precision.HIGHEST)
    back = jnp.einsum("rt,stc->rsc", wave_table[:, half_len:], segments[1:], precision=lax.Precision.HIGHEST)
    stacked = (front + back).reshape(kept_count, 2 * blocks, series.shape[1])
    return jnp.einsum("kbc,kdc->kbd", stacked, stacked, precision=lax.Precision.HIGHEST)


def reduce_kernel(snap_count, cell_count, scale, gram_ref, out_ref, cell_slots, own_cells, snap_slots, own_part, gathered,
                  cell_send, cell_recv, snap_send, snap_recv, gather_send, gather_recv):
    my_snap, my_cell = lax.axis_index("snap"), lax.axis_index("cell")

    def cell_peer(step):
        return lax.rem(my_cell + step, cell_count)

    def snap_peer(step):
        return lax.rem(my_snap + step, snap_count)

    barrier = pltpu.get_barrier_semaphore()
    for step in range(1, cell_count):
        pl.semaphore_signal(barrier, inc=1, device_id=(my_snap, cell_peer(step)), device_id_type=MESH)
    for step in range(1, snap_count):
        pl.semaphore_signal(barrier, inc=1, device_id=(snap_peer(step), my_cell), device_id_type=MESH)
    pl.semaphore_wait(barrier, cell_count + snap_count - 2)

    scatters = [
        pltpu.make_async_remote_copy(
            src_ref=gram_ref.at[cell_peer(step)],
            dst_ref=cell_slots.at[step - 1],
            send_sem=cell_send.at[step - 1],
            recv_sem=cell_recv.at[step - 1],
            device_id=(my_snap, cell_peer(step)),
            device_id_type=MESH,
        )
        for step in range(1, cell_count)
    ]
    for copy in scatters:
        copy.start()
    total = gram_ref[my_cell]
    for step in range(1, cell_count):
        scatters[step - 1].wait_recv()
        total = total + cell_slots[step - 1]
    own_cells[...] = total

    exchanges = [
        pltpu.make_async_remote_copy(
            src_ref=own_cells.at[snap_peer(step)],
            dst_ref=snap_slots.at[step - 1],
            send_sem=snap_send.at[step - 1],
            recv_sem=snap_recv.at[step - 1],
            device_id=(snap_peer(step), my_cell),
            device_id_type=MESH,
        )
        for step in range(1, snap_count)
    ]
    for copy in exchanges:
        copy.start()
    part = own_cells[my_snap]
    for step in range(1, snap_count):
        exchanges[step - 1].wait_recv()
        part = part + snap_slots[step - 1]
    own_part[...] = part * scale

    gathers = [
        pltpu.make_async_remote_copy(
            src_ref=own_part,
            dst_ref=gathered.at[my_cell],
            send_sem=gather_send.at[step - 1],
            recv_sem=gather_recv.at[step - 1],
            device_id=(my_snap, cell_peer(step)),
            device_id_type=MESH,
        )
        for step in range(1, cell_count)
    ]
    for copy in gathers:
        copy.start()
    out_ref[my_cell] = own_part[...]
    for step in range(1, cell_count):
        gathers[step - 1].wait_recv()
        source = lax.rem(my_cell + cell_count - step, cell_count)
        out_ref[source] = gathered[source]
    for copy in scatters + exchanges + gathers:
        copy.wait_send()


def reduce_grams(packed, scale):
    cell_count, snap_count, rows, lanes = packed.shape
    whole_vmem = pl.BlockSpec(memory_space=pltpu.VMEM)
    return pl.pallas_call(
        functools.partial(reduce_kernel, snap_count, cell_count, scale),
        out_shape=jax.ShapeDtypeStruct((cell_count, rows, lanes), jnp.float32),
        in_specs=[whole_vmem],
        out_specs=whole_vmem,
        scratch_shapes=[
            pltpu.VMEM((cell_count - 1, snap_count, rows, lanes), jnp.float32),
            pltpu.VMEM((snap_count, rows, lanes), jnp.float32),
            pltpu.VMEM((snap_count - 1, rows, lanes), jnp.float32),
            pltpu.VMEM((rows, lanes), jnp.float32),
            pltpu.VMEM((cell_count, rows, lanes), jnp.float32),
            pltpu.SemaphoreType.DMA((cell_count - 1,)),
            pltpu.SemaphoreType.DMA((cell_count - 1,)),
            pltpu.SemaphoreType.DMA((snap_count - 1,)),
            pltpu.SemaphoreType.DMA((snap_count - 1,)),
            pltpu.SemaphoreType.DMA((cell_count - 1,)),
            pltpu.SemaphoreType.DMA((cell_count - 1,)),
        ],
        compiler_params=pltpu.CompilerParams(collective_id=0, has_side_effects=True),
    )(packed)


def on_device(pressure, block_starts, retained_bins):
    snap_count = lax.axis_size("snap")
    row_count, width_local = pressure.shape
    pieces = width_local // snap_count
    chunks = max(n for n in range(1, MAX_CHUNKS + 1) if pieces % (n * LANES) == 0)
    wide = pieces // chunks
    wave_table = make_table(retained_bins)
    kept_count = retained_bins.shape[0]
    blocks = block_starts.shape[0]
    received = []
    for i in range(chunks):
        columns = pressure[:, i * snap_count * wide:(i + 1) * snap_count * wide]
        shaped = columns.reshape(row_count, snap_count, wide)
        received.append(lax.all_to_all(shaped, "snap", split_axis=1, concat_axis=0, tiled=True)[:, 0, :])
    products = chunk_products(received[0], wave_table, kept_count, blocks)
    for series in received[1:]:
        products = products + chunk_products(series, wave_table, kept_count, blocks)
    real_part = products[:, :blocks, :blocks] + products[:, blocks:, blocks:]
    imag_part = products[:, :blocks, blocks:] - products[:, blocks:, :blocks]
    lower = jnp.arange(blocks)[:, None] >= jnp.arange(blocks)[None, :]
    halves = jnp.where(lower, real_part, imag_part)
    cell_count = lax.axis_size("cell")
    pairs = kept_count // snap_count // 2
    rows = pairs * blocks // cell_count
    split = halves.reshape(snap_count, 2, pairs, blocks, blocks).transpose(0, 2, 3, 1, 4)
    packed = split.reshape(snap_count, cell_count, rows, 2 * blocks).transpose(1, 0, 2, 3)
    reduced = reduce_grams(packed, 1.0 / (width_local * cell_count))
    joined = reduced.reshape(pairs, blocks, 2, blocks).transpose(2, 0, 1, 3).reshape(2 * pairs, blocks, blocks)
    mirrored = joined.transpose(0, 2, 1)
    diagonal = jnp.eye(blocks, dtype=bool)
    own_real = jnp.where(lower, joined, mirrored)
    own_imag = jnp.where(diagonal, 0.0, jnp.where(lower, -mirrored, joined))
    own_block = jnp.stack([own_real, own_imag], 1)
    order = (block_starts[:, None] // (NFFT // 2) == jnp.arange(blocks)[None, :]).astype(jnp.float32)
    turned = jnp.einsum("kpij,dj->kpid", own_block, order, precision=lax.Precision.HIGHEST)
    return jnp.einsum("bi,kpid->kpbd", order, turned, precision=lax.Precision.HIGHEST)


def solution(mesh):
    placed = (P("snap", "cell"), P(), P())
    return jax.shard_map(
        on_device,
        mesh=mesh,
        in_specs=placed,
        out_specs=P("snap", None, None, None),
        check_vma=False,
    )
```

```python
import functools

import jax
import jax.numpy as jnp
from jax import lax
from jax.experimental import pallas as pl
from jax.experimental.pallas import tpu as pltpu
from jax.sharding import PartitionSpec as P

NFFT = 256
LANES = 128
MESH = pl.DeviceIdType.MESH


def make_table(retained_bins):
    offsets = jnp.arange(NFFT, dtype=jnp.int32)
    window = 0.5 - 0.5 * jnp.cos(2.0 * jnp.pi * offsets.astype(jnp.float32) / NFFT)
    norm_factor = 1.0 / jnp.sqrt(jnp.sum(window * window))
    phase_steps = retained_bins[:, None] * offsets[None, :] % NFFT
    angles = 2.0 * jnp.pi * phase_steps.astype(jnp.float32) / NFFT
    wave_table = jnp.stack(
        [window * norm_factor * jnp.cos(angles), -window * norm_factor * jnp.sin(angles)], 1
    )
    return wave_table.reshape(2 * retained_bins.shape[0], NFFT)


def gather_kernel(snap_count, chunks, wide, kept_count, blocks, pressure_ref, table_ref, out_ref, held, spectra, grams, table_parts,
                  own_sem, send_sem, recv_sem):
    my_snap, my_cell = lax.axis_index("snap"), lax.axis_index("cell")
    row_count = pressure_ref.shape[0]
    half_count = snap_count // 2
    my_half = my_snap // half_count
    half_len = NFFT // 2
    near = [my_half * half_count + lax.rem(my_snap + step, half_count) for step in range(1, half_count)]
    far = [(1 - my_half) * half_count + lax.rem(my_snap + step, half_count) for step in range(half_count)]

    barrier = pltpu.get_barrier_semaphore()
    for peer in near + far:
        pl.semaphore_signal(barrier, inc=1, device_id=(peer, my_cell), device_id_type=MESH)
    pl.semaphore_wait(barrier, snap_count - 1)

    def columns(chunk, owner):
        return pressure_ref.at[:, pl.ds(pl.multiple_of((chunk * snap_count + owner) * wide, wide), wide)]

    def landing(chunk, source):
        return held.at[chunk, pl.ds(pl.multiple_of(source * row_count, 8), row_count)]

    def sending(chunk, peer):
        return pltpu.make_async_remote_copy(
            src_ref=columns(chunk, peer),
            dst_ref=landing(chunk, my_snap),
            send_sem=send_sem.at[chunk, peer],
            recv_sem=recv_sem.at[chunk, my_snap],
            device_id=(peer, my_cell),
            device_id_type=MESH,
        )

    def arriving(chunk, peer):
        return pltpu.make_async_remote_copy(
            src_ref=columns(chunk, peer),
            dst_ref=landing(chunk, peer),
            send_sem=send_sem.at[chunk, peer],
            recv_sem=recv_sem.at[chunk, peer],
            device_id=(peer, my_cell),
            device_id_type=MESH,
        )

    def keeping(chunk):
        return pltpu.make_async_copy(columns(chunk, my_snap), landing(chunk, my_snap), own_sem.at[chunk])

    for chunk in range(chunks):
        for peer in near:
            sending(chunk, peer).start()
        keeping(chunk).start()
    for chunk in range(chunks):
        for peer in far:
            sending(chunk, peer).start()

    table = table_ref[...]
    coarse = table.astype(jnp.bfloat16)
    rows_out = 2 * kept_count
    table_parts[:rows_out] = coarse
    table_parts[rows_out:] = (table - coarse.astype(jnp.float32)).astype(jnp.bfloat16)

    half_rows = snap_count * row_count // 2
    low_count = (half_rows - NFFT) // half_len + 1
    high_start = -(-half_rows // half_len)
    high_count = blocks - high_start

    def transform(chunk, first, count):
        def body(step, carry):
            block = first + step
            data = held[chunk, pl.ds(pl.multiple_of(block * half_len, half_len), NFFT), :]
            data_coarse = data.astype(jnp.bfloat16)
            data_fine = (data - data_coarse.astype(jnp.float32)).astype(jnp.bfloat16)
            both = jnp.dot(table_parts[...], data_coarse, preferred_element_type=jnp.float32)
            rest = jnp.dot(table_parts[:rows_out], data_fine, preferred_element_type=jnp.float32)
            spectra[pl.ds(block, rows_out, stride=blocks), :] = both[:rows_out] + (both[rows_out:] + rest)
            return carry

        lax.fori_loop(0, count, body, 0, unroll=False)

    def product(k):
        data = spectra[pl.ds(pl.multiple_of(k * 2 * blocks, 2 * blocks), 2 * blocks), :]
        data_coarse = data.astype(jnp.bfloat16)
        data_fine = (data - data_coarse.astype(jnp.float32)).astype(jnp.bfloat16)
        left = jnp.concatenate([data_coarse, data_coarse, data_fine], 1)
        right = jnp.concatenate([data_coarse, data_fine, data_coarse], 1)
        return lax.dot_general(left, right, (((1,), (1,)), ((), ())), preferred_element_type=jnp.float32)

    def complex_gram(k):
        whole = grams[k] + product(k) if chunks > 1 else product(k)
        top, turned = whole[:blocks], pltpu.roll(whole[blocks:], blocks, 1)
        lane = lax.broadcasted_iota(jnp.int32, top.shape, 1)
        return jnp.where(lane < blocks, top + turned, top - turned)

    for chunk in range(chunks):
        keeping(chunk).wait()
        for peer in near:
            arriving(chunk, peer).wait_recv()
        transform(chunk, my_half * high_start, low_count + my_half * (high_count - low_count))
        for peer in far:
            arriving(chunk, peer).wait_recv()
        transform(chunk, low_count, high_start - low_count)
        transform(chunk, (1 - my_half) * high_start, high_count + my_half * (low_count - high_count))
        if chunk < chunks - 1:
            def accumulate(k, carry, chunk=chunk):
                grams[k] = product(k) if chunk == 0 else grams[k] + product(k)
                return carry

            lax.fori_loop(0, kept_count, accumulate, 0, unroll=False)

    pairs = kept_count // snap_count // 2

    def finish(place, carry):
        k = place // pairs * (2 * pairs) + lax.rem(place, pairs)
        first, second = complex_gram(k), complex_gram(k + pairs)
        row = lax.broadcasted_iota(jnp.int32, first.shape, 0)
        lane = lax.broadcasted_iota(jnp.int32, first.shape, 1)
        left = jnp.where(row >= lane, first, pltpu.roll(first, blocks, 1))
        right = jnp.where(row >= lane - blocks, pltpu.roll(second, blocks, 1), second)
        out_ref[place] = jnp.where(lane < blocks, left, right)
        return carry

    lax.fori_loop(0, kept_count // 2, finish, 0, unroll=False)
    for chunk in range(chunks):
        for peer in near + far:
            sending(chunk, peer).wait_send()


def local_grams(pressure, wave_table, snap_count, blocks):
    row_count, width_local = pressure.shape
    pieces = width_local // snap_count
    wide = LANES
    chunks = pieces // wide
    kept_count = wave_table.shape[0] // 2
    whole_vmem = pl.BlockSpec(memory_space=pltpu.VMEM)
    return pl.pallas_call(
        functools.partial(gather_kernel, snap_count, chunks, wide, kept_count, blocks),
        out_shape=jax.ShapeDtypeStruct((kept_count // 2, blocks, 2 * blocks), jnp.float32),
        in_specs=[pl.BlockSpec(memory_space=pl.ANY), whole_vmem],
        out_specs=whole_vmem,
        scratch_shapes=[
            pltpu.VMEM((chunks, snap_count * row_count, wide), jnp.float32),
            pltpu.VMEM((2 * kept_count * blocks, wide), jnp.float32),
            pltpu.VMEM((kept_count, 2 * blocks, 2 * blocks), jnp.float32),
            pltpu.VMEM((4 * kept_count, NFFT), jnp.bfloat16),
            pltpu.SemaphoreType.DMA((chunks,)),
            pltpu.SemaphoreType.DMA((chunks, snap_count)),
            pltpu.SemaphoreType.DMA((chunks, snap_count)),
        ],
        compiler_params=pltpu.CompilerParams(collective_id=1, has_side_effects=True),
    )(pressure, wave_table)


def reduce_kernel(snap_count, cell_count, scale, gram_ref, out_ref, cell_slots, own_cells, snap_slots, own_part, gathered,
                  cell_send, cell_recv, snap_send, snap_recv, gather_send, gather_recv):
    my_snap, my_cell = lax.axis_index("snap"), lax.axis_index("cell")

    def cell_peer(step):
        return lax.rem(my_cell + step, cell_count)

    def snap_peer(step):
        return lax.rem(my_snap + step, snap_count)

    barrier = pltpu.get_barrier_semaphore()
    for step in range(1, cell_count):
        pl.semaphore_signal(barrier, inc=1, device_id=(my_snap, cell_peer(step)), device_id_type=MESH)
    for step in range(1, snap_count):
        pl.semaphore_signal(barrier, inc=1, device_id=(snap_peer(step), my_cell), device_id_type=MESH)
    pl.semaphore_wait(barrier, cell_count + snap_count - 2)

    scatters = [
        pltpu.make_async_remote_copy(
            src_ref=gram_ref.at[:, cell_peer(step)],
            dst_ref=cell_slots.at[step - 1],
            send_sem=cell_send.at[step - 1],
            recv_sem=cell_recv.at[step - 1],
            device_id=(my_snap, cell_peer(step)),
            device_id_type=MESH,
        )
        for step in range(1, cell_count)
    ]
    for copy in scatters:
        copy.start()
    total = gram_ref[:, my_cell]
    for step in range(1, cell_count):
        scatters[step - 1].wait_recv()
        total = total + cell_slots[step - 1]
    own_cells[...] = total

    exchanges = [
        pltpu.make_async_remote_copy(
            src_ref=own_cells.at[snap_peer(step)],
            dst_ref=snap_slots.at[step - 1],
            send_sem=snap_send.at[step - 1],
            recv_sem=snap_recv.at[step - 1],
            device_id=(snap_peer(step), my_cell),
            device_id_type=MESH,
        )
        for step in range(1, snap_count)
    ]
    for copy in exchanges:
        copy.start()
    part = own_cells[my_snap]
    for step in range(1, snap_count):
        exchanges[step - 1].wait_recv()
        part = part + snap_slots[step - 1]
    own_part[...] = part * scale

    gathers = [
        pltpu.make_async_remote_copy(
            src_ref=own_part,
            dst_ref=gathered.at[my_cell],
            send_sem=gather_send.at[step - 1],
            recv_sem=gather_recv.at[step - 1],
            device_id=(my_snap, cell_peer(step)),
            device_id_type=MESH,
        )
        for step in range(1, cell_count)
    ]
    for copy in gathers:
        copy.start()
    out_ref[my_cell] = own_part[...]
    for step in range(1, cell_count):
        gathers[step - 1].wait_recv()
        source = lax.rem(my_cell + cell_count - step, cell_count)
        out_ref[source] = gathered[source]
    for copy in scatters + exchanges + gathers:
        copy.wait_send()


def reduce_grams(packed, scale):
    snap_count, cell_count, rows, lanes = packed.shape
    whole_vmem = pl.BlockSpec(memory_space=pltpu.VMEM)
    return pl.pallas_call(
        functools.partial(reduce_kernel, snap_count, cell_count, scale),
        out_shape=jax.ShapeDtypeStruct((cell_count, rows, lanes), jnp.float32),
        in_specs=[whole_vmem],
        out_specs=whole_vmem,
        scratch_shapes=[
            pltpu.VMEM((cell_count - 1, snap_count, rows, lanes), jnp.float32),
            pltpu.VMEM((snap_count, rows, lanes), jnp.float32),
            pltpu.VMEM((snap_count - 1, rows, lanes), jnp.float32),
            pltpu.VMEM((rows, lanes), jnp.float32),
            pltpu.VMEM((cell_count, rows, lanes), jnp.float32),
            pltpu.SemaphoreType.DMA((cell_count - 1,)),
            pltpu.SemaphoreType.DMA((cell_count - 1,)),
            pltpu.SemaphoreType.DMA((snap_count - 1,)),
            pltpu.SemaphoreType.DMA((snap_count - 1,)),
            pltpu.SemaphoreType.DMA((cell_count - 1,)),
            pltpu.SemaphoreType.DMA((cell_count - 1,)),
        ],
        compiler_params=pltpu.CompilerParams(collective_id=0, has_side_effects=True),
    )(packed)


def on_device(pressure, block_starts, retained_bins):
    snap_count = lax.axis_size("snap")
    row_count, width_local = pressure.shape
    kept_count = retained_bins.shape[0]
    blocks = block_starts.shape[0]
    halves = local_grams(pressure, make_table(retained_bins), snap_count, blocks)
    lower = jnp.arange(blocks)[:, None] >= jnp.arange(blocks)[None, :]
    cell_count = lax.axis_size("cell")
    pairs = kept_count // snap_count // 2
    rows = pairs * blocks // cell_count
    packed = halves.reshape(snap_count, cell_count, rows, 2 * blocks)
    reduced = reduce_grams(packed, 1.0 / (width_local * cell_count))
    joined = reduced.reshape(pairs, blocks, 2, blocks).transpose(2, 0, 1, 3).reshape(2 * pairs, blocks, blocks)
    mirrored = joined.transpose(0, 2, 1)
    diagonal = jnp.eye(blocks, dtype=bool)
    own_real = jnp.where(lower, joined, mirrored)
    own_imag = jnp.where(diagonal, 0.0, jnp.where(lower, -mirrored, joined))
    own_block = jnp.stack([own_real, own_imag], 1)
    order = (block_starts[:, None] // (NFFT // 2) == jnp.arange(blocks)[None, :]).astype(jnp.float32)
    turned = jnp.einsum("kpij,dj->kpid", own_block, order, precision=lax.Precision.HIGHEST)
    return jnp.einsum("bi,kpid->kpbd", order, turned, precision=lax.Precision.HIGHEST)


def solution(mesh):
    placed = (P("snap", "cell"), P(), P())
    return jax.shard_map(
        on_device,
        mesh=mesh,
        in_specs=placed,
        out_specs=P("snap", None, None, None),
        check_vma=False,
    )
```

```python
import functools

import jax
import jax.numpy as jnp
from jax import lax
from jax.experimental import pallas as pl
from jax.experimental.pallas import tpu as pltpu
from jax.sharding import PartitionSpec as P

NFFT = 256
LANES = 128
MESH = pl.DeviceIdType.MESH


def make_table(retained_bins):
    offsets = jnp.arange(NFFT, dtype=jnp.int32)
    window = 0.5 - 0.5 * jnp.cos(2.0 * jnp.pi * offsets.astype(jnp.float32) / NFFT)
    norm_factor = 1.0 / jnp.sqrt(jnp.sum(window * window))
    phase_steps = retained_bins[:, None] * offsets[None, :] % NFFT
    angles = 2.0 * jnp.pi * phase_steps.astype(jnp.float32) / NFFT
    return jnp.concatenate([window * norm_factor * jnp.cos(angles), -window * norm_factor * jnp.sin(angles)], 0)


def repeat(count, unroll, step):
    def body(turn, carry):
        for extra in range(unroll):
            step(turn * unroll + extra)
        return carry

    lax.fori_loop(0, count // unroll, body, 0)
    for rest in range(count // unroll * unroll, count):
        step(rest)


def gather_kernel(snap_count, cell_count, chunks, wide, kept_count, blocks, scale, pressure_ref, table_ref, out_ref, held, spectra, grams,
                  table_parts, own_sem, send_sem, recv_sem, *reduction):
    my_snap, my_cell = lax.axis_index("snap"), lax.axis_index("cell")
    row_count = pressure_ref.shape[0]
    half_count = snap_count // 2
    my_half = my_snap // half_count
    half_len = NFFT // 2
    near = [my_half * half_count + lax.rem(my_snap + step, half_count) for step in range(1, half_count)]
    far = [(1 - my_half) * half_count + lax.rem(my_snap + step, half_count) for step in range(half_count)]

    barrier = pltpu.get_barrier_semaphore()
    for peer in near + far:
        pl.semaphore_signal(barrier, inc=1, device_id=(peer, my_cell), device_id_type=MESH)
    if reduction:
        for step in range(1, cell_count):
            pl.semaphore_signal(barrier, inc=1, device_id=(my_snap, lax.rem(my_cell + step, cell_count)), device_id_type=MESH)
    pl.semaphore_wait(barrier, snap_count + cell_count - 2 if reduction else snap_count - 1)

    def columns(chunk, owner):
        return pressure_ref.at[:, pl.ds(pl.multiple_of((chunk * snap_count + owner) * wide, wide), wide)]

    def landing(chunk, source):
        return held.at[chunk, pl.ds(pl.multiple_of(source * row_count, 8), row_count)]

    def sending(chunk, peer):
        return pltpu.make_async_remote_copy(
            src_ref=columns(chunk, peer),
            dst_ref=landing(chunk, my_snap),
            send_sem=send_sem.at[chunk, peer],
            recv_sem=recv_sem.at[chunk, my_snap],
            device_id=(peer, my_cell),
            device_id_type=MESH,
        )

    def arriving(chunk, peer):
        return pltpu.make_async_remote_copy(
            src_ref=columns(chunk, peer),
            dst_ref=landing(chunk, peer),
            send_sem=send_sem.at[chunk, peer],
            recv_sem=recv_sem.at[chunk, peer],
            device_id=(peer, my_cell),
            device_id_type=MESH,
        )

    def keeping(chunk):
        return pltpu.make_async_copy(columns(chunk, my_snap), landing(chunk, my_snap), own_sem.at[chunk])

    for chunk in range(chunks):
        for peer in near:
            sending(chunk, peer).start()
        keeping(chunk).start()
    for chunk in range(chunks):
        for peer in far:
            sending(chunk, peer).start()

    table = table_ref[...]
    coarse = table.astype(jnp.bfloat16)
    rows_out = 2 * kept_count
    table_parts[:rows_out] = coarse
    table_parts[rows_out:] = (table - coarse.astype(jnp.float32)).astype(jnp.bfloat16)

    half_rows = snap_count * row_count // 2
    low_count = (half_rows - NFFT) // half_len + 1
    high_start = -(-half_rows // half_len)
    assert low_count == blocks - high_start

    def transform(chunk, first, count):
        def spread(block, width):
            data = jnp.concatenate(
                [held[chunk, pl.ds(pl.multiple_of((block + i) * half_len, half_len), NFFT), :] for i in range(width)], 1
            )
            data_coarse = data.astype(jnp.bfloat16)
            data_fine = (data - data_coarse.astype(jnp.float32)).astype(jnp.bfloat16)
            both = jnp.dot(table_parts[...], data_coarse, preferred_element_type=jnp.float32)
            rest = jnp.dot(table_parts[:rows_out], data_fine, preferred_element_type=jnp.float32)
            result = both[:rows_out] + (both[rows_out:] + rest)
            for i in range(width):
                spectra[pl.ds(block + i, rows_out, stride=blocks), :] = result[:, i * wide:(i + 1) * wide]

        repeat(count // 2, 2, lambda step: spread(first + 2 * step, 2))
        if count % 2:
            spread(first + count - 1, 1)

    def product(k):
        data = jnp.concatenate(
            [spectra[pl.ds(pl.multiple_of((k + part * kept_count) * blocks, blocks), blocks), :] for part in range(2)], 0
        )
        data_coarse = data.astype(jnp.bfloat16)
        data_fine = (data - data_coarse.astype(jnp.float32)).astype(jnp.bfloat16)
        left = jnp.concatenate([data_coarse, data_coarse, data_fine], 1)
        right = jnp.concatenate([data_coarse, data_fine, data_coarse], 1)
        return lax.dot_general(left, right, (((1,), (1,)), ((), ())), preferred_element_type=jnp.float32)

    def complex_gram(k):
        whole = grams[k] + product(k) if chunks > 1 else product(k)
        top, turned = whole[:blocks], pltpu.roll(whole[blocks:], blocks, 1)
        lane = lax.broadcasted_iota(jnp.int32, top.shape, 1)
        return jnp.where(lane < blocks, top + turned, top - turned)

    for chunk in range(chunks):
        keeping(chunk).wait()
        for peer in near:
            arriving(chunk, peer).wait_recv()
        transform(chunk, my_half * high_start, low_count)
        for peer in far:
            arriving(chunk, peer).wait_recv()
        transform(chunk, low_count, high_start - low_count)
        transform(chunk, (1 - my_half) * high_start, low_count)
        if chunk < chunks - 1:
            def accumulate(k, chunk=chunk):
                grams[k] = product(k) if chunk == 0 else grams[k] + product(k)

            repeat(kept_count, 4, accumulate)

    pairs = kept_count // snap_count // 2

    def finish(place):
        k = place // pairs * (2 * pairs) + lax.rem(place, pairs)
        first, second = complex_gram(k), complex_gram(k + pairs)
        row = lax.broadcasted_iota(jnp.int32, first.shape, 0)
        lane = lax.broadcasted_iota(jnp.int32, first.shape, 1)
        left = jnp.where(row >= lane, first, pltpu.roll(first, blocks, 1))
        right = jnp.where(row >= lane - blocks, pltpu.roll(second, blocks, 1), second)
        return jnp.where(lane < blocks, left, right)

    if not reduction:
        def write(place):
            out_ref[place] = finish(place)

        repeat(kept_count // 2, 2, write)
    else:
        reduce_places(snap_count, cell_count, scale, pairs, blocks, finish, out_ref, *reduction)
    for chunk in range(chunks):
        for peer in near + far:
            sending(chunk, peer).wait_send()


def reduce_places(snap_count, cell_count, scale, pairs, blocks, finish, out_ref, packed, cell_slots, own_cells, snap_slots, own_part,
                  gathered, cell_send, cell_recv, snap_send, snap_recv, gather_send, gather_recv):
    my_snap, my_cell = lax.axis_index("snap"), lax.axis_index("cell")
    rows = own_part.shape[0]

    def cell_peer(step):
        return lax.rem(my_cell + step, cell_count)

    def owner(turn):
        return lax.rem(my_snap + turn + 1, snap_count)

    def share(cell):
        return pl.ds(pl.multiple_of(cell * rows, 8), rows)

    def scattering(turn, step):
        return pltpu.make_async_remote_copy(
            src_ref=packed.at[owner(turn), share(cell_peer(step))],
            dst_ref=cell_slots.at[step - 1, turn],
            send_sem=cell_send.at[step - 1, turn],
            recv_sem=cell_recv.at[step - 1, turn],
            device_id=(my_snap, cell_peer(step)),
            device_id_type=MESH,
        )

    def exchanging(turn):
        return pltpu.make_async_remote_copy(
            src_ref=own_cells.at[turn],
            dst_ref=snap_slots.at[turn],
            send_sem=snap_send.at[turn],
            recv_sem=snap_recv.at[turn],
            device_id=(owner(turn), my_cell),
            device_id_type=MESH,
        )

    def gathering(step):
        return pltpu.make_async_remote_copy(
            src_ref=own_part,
            dst_ref=gathered.at[step - 1],
            send_sem=gather_send.at[step - 1],
            recv_sem=gather_recv.at[step - 1],
            device_id=(my_snap, cell_peer(step)),
            device_id_type=MESH,
        )

    for turn in range(snap_count):
        def write(pair, turn=turn):
            packed[owner(turn), pl.ds(pl.multiple_of(pair * blocks, blocks), blocks)] = finish(owner(turn) * pairs + pair)

        repeat(pairs, 2, write)
        for step in range(1, cell_count):
            scattering(turn, step).start()
    for turn in range(snap_count):
        total = packed[owner(turn), share(my_cell)]
        for step in range(1, cell_count):
            scattering(turn, step).wait_recv()
            total = total + cell_slots[step - 1, turn]
        own_cells[turn] = total
        if turn < snap_count - 1:
            exchanging(turn).start()
    part = own_cells[snap_count - 1]
    for turn in range(snap_count - 1):
        exchanging(turn).wait_recv()
        part = part + snap_slots[turn]
    own_part[...] = part * scale
    for step in range(1, cell_count):
        gathering(step).start()
    out_ref[my_cell] = own_part[...]
    for step in range(1, cell_count):
        gathering(step).wait_recv()
        out_ref[lax.rem(my_cell + cell_count - step, cell_count)] = gathered[step - 1]
    for step in range(1, cell_count):
        gathering(step).wait_send()
        for turn in range(snap_count):
            scattering(turn, step).wait_send()
    for turn in range(snap_count - 1):
        exchanging(turn).wait_send()


def local_grams(pressure, wave_table, snap_count, cell_count, blocks, reduced_rows):
    row_count, width_local = pressure.shape
    pieces = width_local // snap_count
    wide = LANES
    chunks = pieces // wide
    kept_count = wave_table.shape[0] // 2
    whole_vmem = pl.BlockSpec(memory_space=pltpu.VMEM)
    lanes = 2 * blocks
    out_shape, extra = (kept_count // 2, blocks, lanes), []
    if reduced_rows:
        out_shape = (cell_count, reduced_rows, lanes)
        extra = [
            pltpu.VMEM((snap_count, cell_count * reduced_rows, lanes), jnp.float32),
            pltpu.VMEM((cell_count - 1, snap_count, reduced_rows, lanes), jnp.float32),
            pltpu.VMEM((snap_count, reduced_rows, lanes), jnp.float32),
            pltpu.VMEM((snap_count - 1, reduced_rows, lanes), jnp.float32),
            pltpu.VMEM((reduced_rows, lanes), jnp.float32),
            pltpu.VMEM((cell_count - 1, reduced_rows, lanes), jnp.float32),
            pltpu.SemaphoreType.DMA((cell_count - 1, snap_count)),
            pltpu.SemaphoreType.DMA((cell_count - 1, snap_count)),
            pltpu.SemaphoreType.DMA((snap_count - 1,)),
            pltpu.SemaphoreType.DMA((snap_count - 1,)),
            pltpu.SemaphoreType.DMA((cell_count - 1,)),
            pltpu.SemaphoreType.DMA((cell_count - 1,)),
        ]
    scale = 1.0 / (width_local * cell_count)
    return pl.pallas_call(
        functools.partial(gather_kernel, snap_count, cell_count, chunks, wide, kept_count, blocks, scale),
        out_shape=jax.ShapeDtypeStruct(out_shape, jnp.float32),
        in_specs=[pl.BlockSpec(memory_space=pl.ANY), whole_vmem],
        out_specs=whole_vmem,
        scratch_shapes=[
            pltpu.VMEM((chunks, snap_count * row_count, wide), jnp.float32),
            pltpu.VMEM((2 * kept_count * blocks, wide), jnp.float32),
            pltpu.VMEM((kept_count, 2 * blocks, 2 * blocks), jnp.float32),
            pltpu.VMEM((4 * kept_count, NFFT), jnp.bfloat16),
            pltpu.SemaphoreType.DMA((chunks,)),
            pltpu.SemaphoreType.DMA((chunks, snap_count)),
            pltpu.SemaphoreType.DMA((chunks, snap_count)),
            *extra,
        ],
        compiler_params=pltpu.CompilerParams(collective_id=1, has_side_effects=True),
    )(pressure, wave_table)


def reduce_kernel(snap_count, cell_count, scale, gram_ref, out_ref, cell_slots, own_cells, snap_slots, own_part, gathered,
                  cell_send, cell_recv, snap_send, snap_recv, gather_send, gather_recv):
    my_snap, my_cell = lax.axis_index("snap"), lax.axis_index("cell")

    def cell_peer(step):
        return lax.rem(my_cell + step, cell_count)

    def snap_peer(step):
        return lax.rem(my_snap + step, snap_count)

    barrier = pltpu.get_barrier_semaphore()
    for step in range(1, cell_count):
        pl.semaphore_signal(barrier, inc=1, device_id=(my_snap, cell_peer(step)), device_id_type=MESH)
    for step in range(1, snap_count):
        pl.semaphore_signal(barrier, inc=1, device_id=(snap_peer(step), my_cell), device_id_type=MESH)
    pl.semaphore_wait(barrier, cell_count + snap_count - 2)

    scatters = [
        pltpu.make_async_remote_copy(
            src_ref=gram_ref.at[:, cell_peer(step)],
            dst_ref=cell_slots.at[step - 1],
            send_sem=cell_send.at[step - 1],
            recv_sem=cell_recv.at[step - 1],
            device_id=(my_snap, cell_peer(step)),
            device_id_type=MESH,
        )
        for step in range(1, cell_count)
    ]
    for copy in scatters:
        copy.start()
    total = gram_ref[:, my_cell]
    for step in range(1, cell_count):
        scatters[step - 1].wait_recv()
        total = total + cell_slots[step - 1]
    own_cells[...] = total

    exchanges = [
        pltpu.make_async_remote_copy(
            src_ref=own_cells.at[snap_peer(step)],
            dst_ref=snap_slots.at[step - 1],
            send_sem=snap_send.at[step - 1],
            recv_sem=snap_recv.at[step - 1],
            device_id=(snap_peer(step), my_cell),
            device_id_type=MESH,
        )
        for step in range(1, snap_count)
    ]
    for copy in exchanges:
        copy.start()
    part = own_cells[my_snap]
    for step in range(1, snap_count):
        exchanges[step - 1].wait_recv()
        part = part + snap_slots[step - 1]
    own_part[...] = part * scale

    gathers = [
        pltpu.make_async_remote_copy(
            src_ref=own_part,
            dst_ref=gathered.at[my_cell],
            send_sem=gather_send.at[step - 1],
            recv_sem=gather_recv.at[step - 1],
            device_id=(my_snap, cell_peer(step)),
            device_id_type=MESH,
        )
        for step in range(1, cell_count)
    ]
    for copy in gathers:
        copy.start()
    out_ref[my_cell] = own_part[...]
    for step in range(1, cell_count):
        gathers[step - 1].wait_recv()
        source = lax.rem(my_cell + cell_count - step, cell_count)
        out_ref[source] = gathered[source]
    for copy in scatters + exchanges + gathers:
        copy.wait_send()


def reduce_grams(packed, scale):
    snap_count, cell_count, rows, lanes = packed.shape
    whole_vmem = pl.BlockSpec(memory_space=pltpu.VMEM)
    return pl.pallas_call(
        functools.partial(reduce_kernel, snap_count, cell_count, scale),
        out_shape=jax.ShapeDtypeStruct((cell_count, rows, lanes), jnp.float32),
        in_specs=[whole_vmem],
        out_specs=whole_vmem,
        scratch_shapes=[
            pltpu.VMEM((cell_count - 1, snap_count, rows, lanes), jnp.float32),
            pltpu.VMEM((snap_count, rows, lanes), jnp.float32),
            pltpu.VMEM((snap_count - 1, rows, lanes), jnp.float32),
            pltpu.VMEM((rows, lanes), jnp.float32),
            pltpu.VMEM((cell_count, rows, lanes), jnp.float32),
            pltpu.SemaphoreType.DMA((cell_count - 1,)),
            pltpu.SemaphoreType.DMA((cell_count - 1,)),
            pltpu.SemaphoreType.DMA((snap_count - 1,)),
            pltpu.SemaphoreType.DMA((snap_count - 1,)),
            pltpu.SemaphoreType.DMA((cell_count - 1,)),
            pltpu.SemaphoreType.DMA((cell_count - 1,)),
        ],
        compiler_params=pltpu.CompilerParams(collective_id=0, has_side_effects=True),
    )(packed)


def on_device(pressure, block_starts, retained_bins):
    snap_count = lax.axis_size("snap")
    row_count, width_local = pressure.shape
    kept_count = retained_bins.shape[0]
    blocks = block_starts.shape[0]
    lower = jnp.arange(blocks)[:, None] >= jnp.arange(blocks)[None, :]
    cell_count = lax.axis_size("cell")
    pairs = kept_count // snap_count // 2
    rows = pairs * blocks // cell_count
    wave_table = make_table(retained_bins)
    if rows % 8 == 0:
        reduced = local_grams(pressure, wave_table, snap_count, cell_count, blocks, rows)
    else:
        halves = local_grams(pressure, wave_table, snap_count, cell_count, blocks, 0)
        packed = halves.reshape(snap_count, cell_count, rows, 2 * blocks)
        reduced = reduce_grams(packed, 1.0 / (width_local * cell_count))
    joined = reduced.reshape(pairs, blocks, 2, blocks).transpose(2, 0, 1, 3).reshape(2 * pairs, blocks, blocks)
    mirrored = joined.transpose(0, 2, 1)
    diagonal = jnp.eye(blocks, dtype=bool)
    own_real = jnp.where(lower, joined, mirrored)
    own_imag = jnp.where(diagonal, 0.0, jnp.where(lower, -mirrored, joined))
    own_block = jnp.stack([own_real, own_imag], 1)
    order = (block_starts[:, None] // (NFFT // 2) == jnp.arange(blocks)[None, :]).astype(jnp.float32)
    turned = jnp.einsum("kpij,dj->kpid", own_block, order, precision=lax.Precision.HIGHEST)
    return jnp.einsum("bi,kpid->kpbd", order, turned, precision=lax.Precision.HIGHEST)


def solution(mesh):
    placed = (P("snap", "cell"), P(), P())
    return jax.shard_map(
        on_device,
        mesh=mesh,
        in_specs=placed,
        out_specs=P("snap", None, None, None),
        check_vma=False,
    )
```

```python
import functools

import jax
import jax.numpy as jnp
from jax import lax
from jax.experimental import pallas as pl
from jax.experimental.pallas import tpu as pltpu
from jax.sharding import PartitionSpec as P

NFFT = 256
LANES = 128
MESH = pl.DeviceIdType.MESH


def make_table(bins):
    offsets = lax.broadcasted_iota(jnp.int32, (NFFT, bins.shape[1]), 0)
    window = 0.5 - 0.5 * jnp.cos(2.0 * jnp.pi * offsets.astype(jnp.float32) / NFFT)
    norm_factor = 1.0 / jnp.sqrt(jnp.sum(window * window, axis=0, keepdims=True))
    phase_steps = (bins * offsets) & (NFFT - 1)
    angles = 2.0 * jnp.pi * phase_steps.astype(jnp.float32) / NFFT
    return jnp.concatenate([window * norm_factor * jnp.cos(angles), -window * norm_factor * jnp.sin(angles)], 1)


def repeat(count, unroll, step):
    def body(turn, carry):
        for extra in range(unroll):
            step(turn * unroll + extra)
        return carry

    lax.fori_loop(0, count // unroll, body, 0)
    for rest in range(count // unroll * unroll, count):
        step(rest)


def gather_kernel(snap_count, cell_count, chunks, wide, kept_count, blocks, scale, pressure_ref, bins_ref, out_ref, held, spectra, grams,
                  table_parts, own_sem, send_sem, recv_sem, *reduction):
    my_snap, my_cell = lax.axis_index("snap"), lax.axis_index("cell")
    row_count = pressure_ref.shape[0]
    half_count = snap_count // 2
    my_half = my_snap // half_count
    half_len = NFFT // 2
    near = [my_half * half_count + lax.rem(my_snap + step, half_count) for step in range(1, half_count)]
    far = [(1 - my_half) * half_count + lax.rem(my_snap + step, half_count) for step in range(half_count)]

    barrier = pltpu.get_barrier_semaphore()
    for peer in near + far:
        pl.semaphore_signal(barrier, inc=1, device_id=(peer, my_cell), device_id_type=MESH)
    if reduction:
        for step in range(1, cell_count):
            pl.semaphore_signal(barrier, inc=1, device_id=(my_snap, lax.rem(my_cell + step, cell_count)), device_id_type=MESH)
    pl.semaphore_wait(barrier, snap_count + cell_count - 2 if reduction else snap_count - 1)

    def columns(chunk, owner):
        return pressure_ref.at[:, pl.ds(pl.multiple_of((chunk * snap_count + owner) * wide, wide), wide)]

    def landing(chunk, source):
        return held.at[chunk, pl.ds(pl.multiple_of(source * row_count, 8), row_count)]

    def sending(chunk, peer):
        return pltpu.make_async_remote_copy(
            src_ref=columns(chunk, peer),
            dst_ref=landing(chunk, my_snap),
            send_sem=send_sem.at[chunk, peer],
            recv_sem=recv_sem.at[chunk, my_snap],
            device_id=(peer, my_cell),
            device_id_type=MESH,
        )

    def arriving(chunk, peer):
        return pltpu.make_async_remote_copy(
            src_ref=columns(chunk, peer),
            dst_ref=landing(chunk, peer),
            send_sem=send_sem.at[chunk, peer],
            recv_sem=recv_sem.at[chunk, peer],
            device_id=(peer, my_cell),
            device_id_type=MESH,
        )

    def keeping(chunk):
        return pltpu.make_async_copy(columns(chunk, my_snap), landing(chunk, my_snap), own_sem.at[chunk])

    for chunk in range(chunks):
        for peer in near:
            sending(chunk, peer).start()
        keeping(chunk).start()
    for chunk in range(chunks):
        for peer in far:
            sending(chunk, peer).start()

    table = make_table(bins_ref[...]).T
    coarse = table.astype(jnp.bfloat16)
    rows_out = 2 * kept_count
    table_parts[:rows_out] = coarse
    table_parts[rows_out:] = (table - coarse.astype(jnp.float32)).astype(jnp.bfloat16)

    half_rows = snap_count * row_count // 2
    low_count = (half_rows - NFFT) // half_len + 1
    high_start = -(-half_rows // half_len)
    assert low_count == blocks - high_start

    def transform(chunk, first, count):
        def spread(block, width):
            data = jnp.concatenate(
                [held[chunk, pl.ds(pl.multiple_of((block + i) * half_len, half_len), NFFT), :] for i in range(width)], 1
            )
            data_coarse = data.astype(jnp.bfloat16)
            data_fine = (data - data_coarse.astype(jnp.float32)).astype(jnp.bfloat16)
            both = jnp.dot(table_parts[...], data_coarse, preferred_element_type=jnp.float32)
            rest = jnp.dot(table_parts[:rows_out], data_fine, preferred_element_type=jnp.float32)
            result = both[:rows_out] + (both[rows_out:] + rest)
            for i in range(width):
                spectra[pl.ds(block + i, rows_out, stride=blocks), :] = result[:, i * wide:(i + 1) * wide]

        repeat(count // 2, 2, lambda step: spread(first + 2 * step, 2))
        if count % 2:
            spread(first + count - 1, 1)

    def product(k):
        data = jnp.concatenate(
            [spectra[pl.ds(pl.multiple_of((k + part * kept_count) * blocks, blocks), blocks), :] for part in range(2)], 0
        )
        data_coarse = data.astype(jnp.bfloat16)
        data_fine = (data - data_coarse.astype(jnp.float32)).astype(jnp.bfloat16)
        left = jnp.concatenate([data_coarse, data_coarse, data_fine], 1)
        right = jnp.concatenate([data_coarse, data_fine, data_coarse], 1)
        return lax.dot_general(left, right, (((1,), (1,)), ((), ())), preferred_element_type=jnp.float32)

    def complex_gram(k):
        whole = grams[k] + product(k) if chunks > 1 else product(k)
        top, turned = whole[:blocks], pltpu.roll(whole[blocks:], blocks, 1)
        lane = lax.broadcasted_iota(jnp.int32, top.shape, 1)
        return jnp.where(lane < blocks, top + turned, top - turned)

    for chunk in range(chunks):
        keeping(chunk).wait()
        for peer in near:
            arriving(chunk, peer).wait_recv()
        transform(chunk, my_half * high_start, low_count)
        for peer in far:
            arriving(chunk, peer).wait_recv()
        transform(chunk, low_count, high_start - low_count)
        transform(chunk, (1 - my_half) * high_start, low_count)
        if chunk < chunks - 1:
            def accumulate(k, chunk=chunk):
                grams[k] = product(k) if chunk == 0 else grams[k] + product(k)

            repeat(kept_count, 4, accumulate)

    pairs = kept_count // snap_count // 2

    def finish(place):
        k = place // pairs * (2 * pairs) + lax.rem(place, pairs)
        first, second = complex_gram(k), complex_gram(k + pairs)
        row = lax.broadcasted_iota(jnp.int32, first.shape, 0)
        lane = lax.broadcasted_iota(jnp.int32, first.shape, 1)
        left = jnp.where(row >= lane, first, pltpu.roll(first, blocks, 1))
        right = jnp.where(row >= lane - blocks, pltpu.roll(second, blocks, 1), second)
        return jnp.where(lane < blocks, left, right)

    if not reduction:
        def write(place):
            out_ref[place] = finish(place)

        repeat(kept_count // 2, 2, write)
    else:
        reduce_places(snap_count, cell_count, scale, pairs, blocks, finish, out_ref, *reduction)
    for chunk in range(chunks):
        for peer in near + far:
            sending(chunk, peer).wait_send()


def reduce_places(snap_count, cell_count, scale, pairs, blocks, finish, out_ref, packed, cell_slots, own_cells, snap_slots, own_part,
                  gathered, cell_send, cell_recv, snap_send, snap_recv, gather_send, gather_recv):
    my_snap, my_cell = lax.axis_index("snap"), lax.axis_index("cell")
    rows = own_part.shape[0]

    def cell_peer(step):
        return lax.rem(my_cell + step, cell_count)

    def owner(turn):
        return lax.rem(my_snap + turn + 1, snap_count)

    def share(cell):
        return pl.ds(pl.multiple_of(cell * rows, 8), rows)

    def scattering(turn, step):
        return pltpu.make_async_remote_copy(
            src_ref=packed.at[owner(turn), share(cell_peer(step))],
            dst_ref=cell_slots.at[step - 1, turn],
            send_sem=cell_send.at[step - 1, turn],
            recv_sem=cell_recv.at[step - 1, turn],
            device_id=(my_snap, cell_peer(step)),
            device_id_type=MESH,
        )

    def exchanging(turn):
        return pltpu.make_async_remote_copy(
            src_ref=own_cells.at[turn],
            dst_ref=snap_slots.at[turn],
            send_sem=snap_send.at[turn],
            recv_sem=snap_recv.at[turn],
            device_id=(owner(turn), my_cell),
            device_id_type=MESH,
        )

    def gathering(step):
        return pltpu.make_async_remote_copy(
            src_ref=own_part,
            dst_ref=gathered.at[step - 1],
            send_sem=gather_send.at[step - 1],
            recv_sem=gather_recv.at[step - 1],
            device_id=(my_snap, cell_peer(step)),
            device_id_type=MESH,
        )

    for turn in range(snap_count):
        def write(pair, turn=turn):
            packed[owner(turn), pl.ds(pl.multiple_of(pair * blocks, blocks), blocks)] = finish(owner(turn) * pairs + pair)

        repeat(pairs, 2, write)
        for step in range(1, cell_count):
            scattering(turn, step).start()
    for turn in range(snap_count):
        total = packed[owner(turn), share(my_cell)]
        for step in range(1, cell_count):
            scattering(turn, step).wait_recv()
            total = total + cell_slots[step - 1, turn]
        own_cells[turn] = total
        if turn < snap_count - 1:
            exchanging(turn).start()
    part = own_cells[snap_count - 1]
    for turn in range(snap_count - 1):
        exchanging(turn).wait_recv()
        part = part + snap_slots[turn]
    own_part[...] = part * scale
    for step in range(1, cell_count):
        gathering(step).start()
    out_ref[my_cell] = own_part[...]
    for step in range(1, cell_count):
        gathering(step).wait_recv()
        out_ref[lax.rem(my_cell + cell_count - step, cell_count)] = gathered[step - 1]
    for step in range(1, cell_count):
        gathering(step).wait_send()
        for turn in range(snap_count):
            scattering(turn, step).wait_send()
    for turn in range(snap_count - 1):
        exchanging(turn).wait_send()


def local_grams(pressure, retained_bins, snap_count, cell_count, blocks, reduced_rows):
    row_count, width_local = pressure.shape
    pieces = width_local // snap_count
    wide = LANES
    chunks = pieces // wide
    kept_count = retained_bins.shape[0]
    whole_vmem = pl.BlockSpec(memory_space=pltpu.VMEM)
    lanes = 2 * blocks
    out_shape, extra = (kept_count // 2, blocks, lanes), []
    if reduced_rows:
        out_shape = (cell_count, reduced_rows, lanes)
        extra = [
            pltpu.VMEM((snap_count, cell_count * reduced_rows, lanes), jnp.float32),
            pltpu.VMEM((cell_count - 1, snap_count, reduced_rows, lanes), jnp.float32),
            pltpu.VMEM((snap_count, reduced_rows, lanes), jnp.float32),
            pltpu.VMEM((snap_count - 1, reduced_rows, lanes), jnp.float32),
            pltpu.VMEM((reduced_rows, lanes), jnp.float32),
            pltpu.VMEM((cell_count - 1, reduced_rows, lanes), jnp.float32),
            pltpu.SemaphoreType.DMA((cell_count - 1, snap_count)),
            pltpu.SemaphoreType.DMA((cell_count - 1, snap_count)),
            pltpu.SemaphoreType.DMA((snap_count - 1,)),
            pltpu.SemaphoreType.DMA((snap_count - 1,)),
            pltpu.SemaphoreType.DMA((cell_count - 1,)),
            pltpu.SemaphoreType.DMA((cell_count - 1,)),
        ]
    scale = 1.0 / (width_local * cell_count)
    return pl.pallas_call(
        functools.partial(gather_kernel, snap_count, cell_count, chunks, wide, kept_count, blocks, scale),
        out_shape=jax.ShapeDtypeStruct(out_shape, jnp.float32),
        in_specs=[pl.BlockSpec(memory_space=pl.ANY), whole_vmem],
        out_specs=whole_vmem,
        scratch_shapes=[
            pltpu.VMEM((chunks, snap_count * row_count, wide), jnp.float32),
            pltpu.VMEM((2 * kept_count * blocks, wide), jnp.float32),
            pltpu.VMEM((kept_count, 2 * blocks, 2 * blocks), jnp.float32),
            pltpu.VMEM((4 * kept_count, NFFT), jnp.bfloat16),
            pltpu.SemaphoreType.DMA((chunks,)),
            pltpu.SemaphoreType.DMA((chunks, snap_count)),
            pltpu.SemaphoreType.DMA((chunks, snap_count)),
            *extra,
        ],
        compiler_params=pltpu.CompilerParams(collective_id=1, has_side_effects=True),
    )(pressure, retained_bins.reshape(1, kept_count))


def reduce_kernel(snap_count, cell_count, scale, gram_ref, out_ref, cell_slots, own_cells, snap_slots, own_part, gathered,
                  cell_send, cell_recv, snap_send, snap_recv, gather_send, gather_recv):
    my_snap, my_cell = lax.axis_index("snap"), lax.axis_index("cell")

    def cell_peer(step):
        return lax.rem(my_cell + step, cell_count)

    def snap_peer(step):
        return lax.rem(my_snap + step, snap_count)

    barrier = pltpu.get_barrier_semaphore()
    for step in range(1, cell_count):
        pl.semaphore_signal(barrier, inc=1, device_id=(my_snap, cell_peer(step)), device_id_type=MESH)
    for step in range(1, snap_count):
        pl.semaphore_signal(barrier, inc=1, device_id=(snap_peer(step), my_cell), device_id_type=MESH)
    pl.semaphore_wait(barrier, cell_count + snap_count - 2)

    scatters = [
        pltpu.make_async_remote_copy(
            src_ref=gram_ref.at[:, cell_peer(step)],
            dst_ref=cell_slots.at[step - 1],
            send_sem=cell_send.at[step - 1],
            recv_sem=cell_recv.at[step - 1],
            device_id=(my_snap, cell_peer(step)),
            device_id_type=MESH,
        )
        for step in range(1, cell_count)
    ]
    for copy in scatters:
        copy.start()
    total = gram_ref[:, my_cell]
    for step in range(1, cell_count):
        scatters[step - 1].wait_recv()
        total = total + cell_slots[step - 1]
    own_cells[...] = total

    exchanges = [
        pltpu.make_async_remote_copy(
            src_ref=own_cells.at[snap_peer(step)],
            dst_ref=snap_slots.at[step - 1],
            send_sem=snap_send.at[step - 1],
            recv_sem=snap_recv.at[step - 1],
            device_id=(snap_peer(step), my_cell),
            device_id_type=MESH,
        )
        for step in range(1, snap_count)
    ]
    for copy in exchanges:
        copy.start()
    part = own_cells[my_snap]
    for step in range(1, snap_count):
        exchanges[step - 1].wait_recv()
        part = part + snap_slots[step - 1]
    own_part[...] = part * scale

    gathers = [
        pltpu.make_async_remote_copy(
            src_ref=own_part,
            dst_ref=gathered.at[my_cell],
            send_sem=gather_send.at[step - 1],
            recv_sem=gather_recv.at[step - 1],
            device_id=(my_snap, cell_peer(step)),
            device_id_type=MESH,
        )
        for step in range(1, cell_count)
    ]
    for copy in gathers:
        copy.start()
    out_ref[my_cell] = own_part[...]
    for step in range(1, cell_count):
        gathers[step - 1].wait_recv()
        source = lax.rem(my_cell + cell_count - step, cell_count)
        out_ref[source] = gathered[source]
    for copy in scatters + exchanges + gathers:
        copy.wait_send()


def reduce_grams(packed, scale):
    snap_count, cell_count, rows, lanes = packed.shape
    whole_vmem = pl.BlockSpec(memory_space=pltpu.VMEM)
    return pl.pallas_call(
        functools.partial(reduce_kernel, snap_count, cell_count, scale),
        out_shape=jax.ShapeDtypeStruct((cell_count, rows, lanes), jnp.float32),
        in_specs=[whole_vmem],
        out_specs=whole_vmem,
        scratch_shapes=[
            pltpu.VMEM((cell_count - 1, snap_count, rows, lanes), jnp.float32),
            pltpu.VMEM((snap_count, rows, lanes), jnp.float32),
            pltpu.VMEM((snap_count - 1, rows, lanes), jnp.float32),
            pltpu.VMEM((rows, lanes), jnp.float32),
            pltpu.VMEM((cell_count, rows, lanes), jnp.float32),
            pltpu.SemaphoreType.DMA((cell_count - 1,)),
            pltpu.SemaphoreType.DMA((cell_count - 1,)),
            pltpu.SemaphoreType.DMA((snap_count - 1,)),
            pltpu.SemaphoreType.DMA((snap_count - 1,)),
            pltpu.SemaphoreType.DMA((cell_count - 1,)),
            pltpu.SemaphoreType.DMA((cell_count - 1,)),
        ],
        compiler_params=pltpu.CompilerParams(collective_id=0, has_side_effects=True),
    )(packed)


def on_device(pressure, block_starts, retained_bins):
    snap_count = lax.axis_size("snap")
    row_count, width_local = pressure.shape
    kept_count = retained_bins.shape[0]
    blocks = block_starts.shape[0]
    lower = jnp.arange(blocks)[:, None] >= jnp.arange(blocks)[None, :]
    cell_count = lax.axis_size("cell")
    pairs = kept_count // snap_count // 2
    rows = pairs * blocks // cell_count
    if rows % 8 == 0:
        reduced = local_grams(pressure, retained_bins, snap_count, cell_count, blocks, rows)
    else:
        halves = local_grams(pressure, retained_bins, snap_count, cell_count, blocks, 0)
        packed = halves.reshape(snap_count, cell_count, rows, 2 * blocks)
        reduced = reduce_grams(packed, 1.0 / (width_local * cell_count))
    paired = reduced.reshape(pairs, blocks, 2 * blocks)
    joined = jnp.concatenate([paired[:, :, :blocks], paired[:, :, blocks:]], 0)
    mirrored = joined.transpose(0, 2, 1)
    diagonal = jnp.eye(blocks, dtype=bool)
    own_real = jnp.where(lower, joined, mirrored)
    own_imag = jnp.where(diagonal, 0.0, jnp.where(lower, -mirrored, joined))
    own_block = jnp.stack([own_real, own_imag], 1)
    order = (block_starts[:, None] // (NFFT // 2) == jnp.arange(blocks)[None, :]).astype(jnp.float32)
    turned = jnp.einsum("kpij,dj->kpid", own_block, order, precision=lax.Precision.HIGHEST)
    return jnp.einsum("bi,kpid->kpbd", order, turned, precision=lax.Precision.HIGHEST)


def solution(mesh):
    placed = (P("snap", "cell"), P(), P())
    return jax.shard_map(
        on_device,
        mesh=mesh,
        in_specs=placed,
        out_specs=P("snap", None, None, None),
        check_vma=False,
    )
```

```python
import functools

import jax
import jax.numpy as jnp
from jax import lax
from jax.experimental import pallas as pl
from jax.experimental.pallas import tpu as pltpu
from jax.sharding import PartitionSpec as P

NFFT = 256
LANES = 128
MESH = pl.DeviceIdType.MESH


def make_table(bins):
    offsets = lax.broadcasted_iota(jnp.int32, (NFFT, bins.shape[1]), 0)
    window = 0.5 - 0.5 * jnp.cos(2.0 * jnp.pi * offsets.astype(jnp.float32) / NFFT)
    norm_factor = 1.0 / jnp.sqrt(jnp.sum(window * window, axis=0, keepdims=True))
    phase_steps = (bins * offsets) & (NFFT - 1)
    angles = 2.0 * jnp.pi * phase_steps.astype(jnp.float32) / NFFT
    return jnp.concatenate([window * norm_factor * jnp.cos(angles), -window * norm_factor * jnp.sin(angles)], 1)


def repeat(count, unroll, step):
    def body(turn, carry):
        for extra in range(unroll):
            step(turn * unroll + extra)
        return carry

    lax.fori_loop(0, count // unroll, body, 0)
    for rest in range(count // unroll * unroll, count):
        step(rest)


def gather_kernel(snap_count, cell_count, chunks, wide, kept_count, blocks, scale, pressure_ref, bins_ref, out_ref, held, spectra, grams,
                  table_parts, own_sem, send_sem, recv_sem, *reduction):
    my_snap, my_cell = lax.axis_index("snap"), lax.axis_index("cell")
    row_count = pressure_ref.shape[0]
    half_count = snap_count // 2
    my_half = my_snap // half_count
    half_len = NFFT // 2
    near = [my_half * half_count + lax.rem(my_snap + step, half_count) for step in range(1, half_count)]
    far = [(1 - my_half) * half_count + lax.rem(my_snap + step, half_count) for step in range(half_count)]

    barrier = pltpu.get_barrier_semaphore()
    for peer in near + far:
        pl.semaphore_signal(barrier, inc=1, device_id=(peer, my_cell), device_id_type=MESH)
    if reduction:
        for step in range(1, cell_count):
            pl.semaphore_signal(barrier, inc=1, device_id=(my_snap, lax.rem(my_cell + step, cell_count)), device_id_type=MESH)
    pl.semaphore_wait(barrier, snap_count + cell_count - 2 if reduction else snap_count - 1)

    def columns(chunk, owner):
        return pressure_ref.at[:, pl.ds(pl.multiple_of((chunk * snap_count + owner) * wide, wide), wide)]

    def landing(chunk, source):
        return held.at[chunk, pl.ds(pl.multiple_of(source * row_count, 8), row_count)]

    def sending(chunk, peer):
        return pltpu.make_async_remote_copy(
            src_ref=columns(chunk, peer),
            dst_ref=landing(chunk, my_snap),
            send_sem=send_sem.at[chunk, peer],
            recv_sem=recv_sem.at[chunk, my_snap],
            device_id=(peer, my_cell),
            device_id_type=MESH,
        )

    def arriving(chunk, peer):
        return pltpu.make_async_remote_copy(
            src_ref=columns(chunk, peer),
            dst_ref=landing(chunk, peer),
            send_sem=send_sem.at[chunk, peer],
            recv_sem=recv_sem.at[chunk, peer],
            device_id=(peer, my_cell),
            device_id_type=MESH,
        )

    def keeping(chunk):
        return pltpu.make_async_copy(columns(chunk, my_snap), landing(chunk, my_snap), own_sem.at[chunk])

    for chunk in range(chunks):
        for peer in near:
            sending(chunk, peer).start()
        keeping(chunk).start()
    for chunk in range(chunks):
        for peer in far:
            sending(chunk, peer).start()

    table = make_table(bins_ref[...]).T
    coarse = table.astype(jnp.bfloat16)
    rows_out = 2 * kept_count
    table_parts[:rows_out] = coarse
    table_parts[rows_out:] = (table - coarse.astype(jnp.float32)).astype(jnp.bfloat16)

    half_rows = snap_count * row_count // 2
    low_count = (half_rows - NFFT) // half_len + 1
    high_start = -(-half_rows // half_len)
    assert low_count == blocks - high_start

    def transform(chunk, first, count):
        def spread(block, width):
            data = jnp.concatenate(
                [held[chunk, pl.ds(pl.multiple_of((block + i) * half_len, half_len), NFFT), :] for i in range(width)], 1
            )
            data_coarse = data.astype(jnp.bfloat16)
            data_fine = (data - data_coarse.astype(jnp.float32)).astype(jnp.bfloat16)
            both = jnp.dot(table_parts[...], data_coarse, preferred_element_type=jnp.float32)
            rest = jnp.dot(table_parts[:rows_out], data_fine, preferred_element_type=jnp.float32)
            result = both[:rows_out] + (both[rows_out:] + rest)
            for i in range(width):
                spectra[pl.ds(block + i, rows_out, stride=blocks), :] = result[:, i * wide:(i + 1) * wide]

        repeat(count // 2, 2, lambda step: spread(first + 2 * step, 2))
        if count % 2:
            spread(first + count - 1, 1)

    def product(k):
        data = jnp.concatenate(
            [spectra[pl.ds(pl.multiple_of((k + part * kept_count) * blocks, blocks), blocks), :] for part in range(2)], 0
        )
        data_coarse = data.astype(jnp.bfloat16)
        data_fine = (data - data_coarse.astype(jnp.float32)).astype(jnp.bfloat16)
        right = jnp.concatenate([data_coarse, data_fine], 0)
        both = lax.dot_general(data_coarse, right, (((1,), (1,)), ((), ())), preferred_element_type=jnp.float32)
        cross = both[:, 2 * blocks:]
        return both[:, :2 * blocks] + (cross + cross.T)

    def complex_gram(k):
        whole = grams[k] + product(k) if chunks > 1 else product(k)
        top, turned = whole[:blocks], pltpu.roll(whole[blocks:], blocks, 1)
        lane = lax.broadcasted_iota(jnp.int32, top.shape, 1)
        return jnp.where(lane < blocks, top + turned, top - turned)

    for chunk in range(chunks):
        keeping(chunk).wait()
        for peer in near:
            arriving(chunk, peer).wait_recv()
        transform(chunk, my_half * high_start, low_count)
        for peer in far:
            arriving(chunk, peer).wait_recv()
        transform(chunk, low_count, high_start - low_count)
        transform(chunk, (1 - my_half) * high_start, low_count)
        if chunk < chunks - 1:
            def accumulate(k, chunk=chunk):
                grams[k] = product(k) if chunk == 0 else grams[k] + product(k)

            repeat(kept_count, 4, accumulate)

    pairs = kept_count // snap_count // 2

    def finish(place):
        k = place // pairs * (2 * pairs) + lax.rem(place, pairs)
        first, second = complex_gram(k), complex_gram(k + pairs)
        row = lax.broadcasted_iota(jnp.int32, first.shape, 0)
        lane = lax.broadcasted_iota(jnp.int32, first.shape, 1)
        left = jnp.where(row >= lane, first, pltpu.roll(first, blocks, 1))
        right = jnp.where(row >= lane - blocks, pltpu.roll(second, blocks, 1), second)
        return jnp.where(lane < blocks, left, right)

    if not reduction:
        def write(place):
            out_ref[place] = finish(place)

        repeat(kept_count // 2, 2, write)
    else:
        reduce_places(snap_count, cell_count, scale, pairs, blocks, finish, out_ref, *reduction)
    for chunk in range(chunks):
        for peer in near + far:
            sending(chunk, peer).wait_send()


def reduce_places(snap_count, cell_count, scale, pairs, blocks, finish, out_ref, packed, cell_slots, own_cells, snap_slots, own_part,
                  gathered, cell_send, cell_recv, snap_send, snap_recv, gather_send, gather_recv):
    my_snap, my_cell = lax.axis_index("snap"), lax.axis_index("cell")
    rows = own_part.shape[0]

    def cell_peer(step):
        return lax.rem(my_cell + step, cell_count)

    def owner(turn):
        return lax.rem(my_snap + turn + 1, snap_count)

    def share(cell):
        return pl.ds(pl.multiple_of(cell * rows, 8), rows)

    def scattering(turn, step):
        return pltpu.make_async_remote_copy(
            src_ref=packed.at[owner(turn), share(cell_peer(step))],
            dst_ref=cell_slots.at[step - 1, turn],
            send_sem=cell_send.at[step - 1, turn],
            recv_sem=cell_recv.at[step - 1, turn],
            device_id=(my_snap, cell_peer(step)),
            device_id_type=MESH,
        )

    def exchanging(turn):
        return pltpu.make_async_remote_copy(
            src_ref=own_cells.at[turn],
            dst_ref=snap_slots.at[turn],
            send_sem=snap_send.at[turn],
            recv_sem=snap_recv.at[turn],
            device_id=(owner(turn), my_cell),
            device_id_type=MESH,
        )

    def gathering(step):
        return pltpu.make_async_remote_copy(
            src_ref=own_part,
            dst_ref=gathered.at[step - 1],
            send_sem=gather_send.at[step - 1],
            recv_sem=gather_recv.at[step - 1],
            device_id=(my_snap, cell_peer(step)),
            device_id_type=MESH,
        )

    for turn in range(snap_count):
        def write(pair, turn=turn):
            packed[owner(turn), pl.ds(pl.multiple_of(pair * blocks, blocks), blocks)] = finish(owner(turn) * pairs + pair)

        repeat(pairs, 2, write)
        for step in range(1, cell_count):
            scattering(turn, step).start()
    for turn in range(snap_count):
        total = packed[owner(turn), share(my_cell)]
        for step in range(1, cell_count):
            scattering(turn, step).wait_recv()
            total = total + cell_slots[step - 1, turn]
        own_cells[turn] = total
        if turn < snap_count - 1:
            exchanging(turn).start()
    part = own_cells[snap_count - 1]
    for turn in range(snap_count - 1):
        exchanging(turn).wait_recv()
        part = part + snap_slots[turn]
    own_part[...] = part * scale
    for step in range(1, cell_count):
        gathering(step).start()
    out_ref[my_cell] = own_part[...]
    for step in range(1, cell_count):
        gathering(step).wait_recv()
        out_ref[lax.rem(my_cell + cell_count - step, cell_count)] = gathered[step - 1]
    for step in range(1, cell_count):
        gathering(step).wait_send()
        for turn in range(snap_count):
            scattering(turn, step).wait_send()
    for turn in range(snap_count - 1):
        exchanging(turn).wait_send()


def local_grams(pressure, retained_bins, snap_count, cell_count, blocks, reduced_rows):
    row_count, width_local = pressure.shape
    pieces = width_local // snap_count
    wide = LANES
    chunks = pieces // wide
    kept_count = retained_bins.shape[0]
    whole_vmem = pl.BlockSpec(memory_space=pltpu.VMEM)
    lanes = 2 * blocks
    out_shape, extra = (kept_count // 2, blocks, lanes), []
    if reduced_rows:
        out_shape = (cell_count, reduced_rows, lanes)
        extra = [
            pltpu.VMEM((snap_count, cell_count * reduced_rows, lanes), jnp.float32),
            pltpu.VMEM((cell_count - 1, snap_count, reduced_rows, lanes), jnp.float32),
            pltpu.VMEM((snap_count, reduced_rows, lanes), jnp.float32),
            pltpu.VMEM((snap_count - 1, reduced_rows, lanes), jnp.float32),
            pltpu.VMEM((reduced_rows, lanes), jnp.float32),
            pltpu.VMEM((cell_count - 1, reduced_rows, lanes), jnp.float32),
            pltpu.SemaphoreType.DMA((cell_count - 1, snap_count)),
            pltpu.SemaphoreType.DMA((cell_count - 1, snap_count)),
            pltpu.SemaphoreType.DMA((snap_count - 1,)),
            pltpu.SemaphoreType.DMA((snap_count - 1,)),
            pltpu.SemaphoreType.DMA((cell_count - 1,)),
            pltpu.SemaphoreType.DMA((cell_count - 1,)),
        ]
    scale = 1.0 / (width_local * cell_count)
    return pl.pallas_call(
        functools.partial(gather_kernel, snap_count, cell_count, chunks, wide, kept_count, blocks, scale),
        out_shape=jax.ShapeDtypeStruct(out_shape, jnp.float32),
        in_specs=[pl.BlockSpec(memory_space=pl.ANY), whole_vmem],
        out_specs=whole_vmem,
        scratch_shapes=[
            pltpu.VMEM((chunks, snap_count * row_count, wide), jnp.float32),
            pltpu.VMEM((2 * kept_count * blocks, wide), jnp.float32),
            pltpu.VMEM((kept_count, 2 * blocks, 2 * blocks), jnp.float32),
            pltpu.VMEM((4 * kept_count, NFFT), jnp.bfloat16),
            pltpu.SemaphoreType.DMA((chunks,)),
            pltpu.SemaphoreType.DMA((chunks, snap_count)),
            pltpu.SemaphoreType.DMA((chunks, snap_count)),
            *extra,
        ],
        compiler_params=pltpu.CompilerParams(collective_id=1, has_side_effects=True),
    )(pressure, retained_bins.reshape(1, kept_count))


def reduce_kernel(snap_count, cell_count, scale, gram_ref, out_ref, cell_slots, own_cells, snap_slots, own_part, gathered,
                  cell_send, cell_recv, snap_send, snap_recv, gather_send, gather_recv):
    my_snap, my_cell = lax.axis_index("snap"), lax.axis_index("cell")

    def cell_peer(step):
        return lax.rem(my_cell + step, cell_count)

    def snap_peer(step):
        return lax.rem(my_snap + step, snap_count)

    barrier = pltpu.get_barrier_semaphore()
    for step in range(1, cell_count):
        pl.semaphore_signal(barrier, inc=1, device_id=(my_snap, cell_peer(step)), device_id_type=MESH)
    for step in range(1, snap_count):
        pl.semaphore_signal(barrier, inc=1, device_id=(snap_peer(step), my_cell), device_id_type=MESH)
    pl.semaphore_wait(barrier, cell_count + snap_count - 2)

    scatters = [
        pltpu.make_async_remote_copy(
            src_ref=gram_ref.at[:, cell_peer(step)],
            dst_ref=cell_slots.at[step - 1],
            send_sem=cell_send.at[step - 1],
            recv_sem=cell_recv.at[step - 1],
            device_id=(my_snap, cell_peer(step)),
            device_id_type=MESH,
        )
        for step in range(1, cell_count)
    ]
    for copy in scatters:
        copy.start()
    total = gram_ref[:, my_cell]
    for step in range(1, cell_count):
        scatters[step - 1].wait_recv()
        total = total + cell_slots[step - 1]
    own_cells[...] = total

    exchanges = [
        pltpu.make_async_remote_copy(
            src_ref=own_cells.at[snap_peer(step)],
            dst_ref=snap_slots.at[step - 1],
            send_sem=snap_send.at[step - 1],
            recv_sem=snap_recv.at[step - 1],
            device_id=(snap_peer(step), my_cell),
            device_id_type=MESH,
        )
        for step in range(1, snap_count)
    ]
    for copy in exchanges:
        copy.start()
    part = own_cells[my_snap]
    for step in range(1, snap_count):
        exchanges[step - 1].wait_recv()
        part = part + snap_slots[step - 1]
    own_part[...] = part * scale

    gathers = [
        pltpu.make_async_remote_copy(
            src_ref=own_part,
            dst_ref=gathered.at[my_cell],
            send_sem=gather_send.at[step - 1],
            recv_sem=gather_recv.at[step - 1],
            device_id=(my_snap, cell_peer(step)),
            device_id_type=MESH,
        )
        for step in range(1, cell_count)
    ]
    for copy in gathers:
        copy.start()
    out_ref[my_cell] = own_part[...]
    for step in range(1, cell_count):
        gathers[step - 1].wait_recv()
        source = lax.rem(my_cell + cell_count - step, cell_count)
        out_ref[source] = gathered[source]
    for copy in scatters + exchanges + gathers:
        copy.wait_send()


def reduce_grams(packed, scale):
    snap_count, cell_count, rows, lanes = packed.shape
    whole_vmem = pl.BlockSpec(memory_space=pltpu.VMEM)
    return pl.pallas_call(
        functools.partial(reduce_kernel, snap_count, cell_count, scale),
        out_shape=jax.ShapeDtypeStruct((cell_count, rows, lanes), jnp.float32),
        in_specs=[whole_vmem],
        out_specs=whole_vmem,
        scratch_shapes=[
            pltpu.VMEM((cell_count - 1, snap_count, rows, lanes), jnp.float32),
            pltpu.VMEM((snap_count, rows, lanes), jnp.float32),
            pltpu.VMEM((snap_count - 1, rows, lanes), jnp.float32),
            pltpu.VMEM((rows, lanes), jnp.float32),
            pltpu.VMEM((cell_count, rows, lanes), jnp.float32),
            pltpu.SemaphoreType.DMA((cell_count - 1,)),
            pltpu.SemaphoreType.DMA((cell_count - 1,)),
            pltpu.SemaphoreType.DMA((snap_count - 1,)),
            pltpu.SemaphoreType.DMA((snap_count - 1,)),
            pltpu.SemaphoreType.DMA((cell_count - 1,)),
            pltpu.SemaphoreType.DMA((cell_count - 1,)),
        ],
        compiler_params=pltpu.CompilerParams(collective_id=0, has_side_effects=True),
    )(packed)


def on_device(pressure, block_starts, retained_bins):
    snap_count = lax.axis_size("snap")
    row_count, width_local = pressure.shape
    kept_count = retained_bins.shape[0]
    blocks = block_starts.shape[0]
    lower = jnp.arange(blocks)[:, None] >= jnp.arange(blocks)[None, :]
    cell_count = lax.axis_size("cell")
    pairs = kept_count // snap_count // 2
    rows = pairs * blocks // cell_count
    if rows % 8 == 0:
        reduced = local_grams(pressure, retained_bins, snap_count, cell_count, blocks, rows)
    else:
        halves = local_grams(pressure, retained_bins, snap_count, cell_count, blocks, 0)
        packed = halves.reshape(snap_count, cell_count, rows, 2 * blocks)
        reduced = reduce_grams(packed, 1.0 / (width_local * cell_count))
    paired = reduced.reshape(pairs, blocks, 2 * blocks)
    joined = jnp.concatenate([paired[:, :, :blocks], paired[:, :, blocks:]], 0)
    mirrored = joined.transpose(0, 2, 1)
    diagonal = jnp.eye(blocks, dtype=bool)
    own_real = jnp.where(lower, joined, mirrored)
    own_imag = jnp.where(diagonal, 0.0, jnp.where(lower, -mirrored, joined))
    own_block = jnp.stack([own_real, own_imag], 1)
    order = (block_starts[:, None] // (NFFT // 2) == jnp.arange(blocks)[None, :]).astype(jnp.float32)
    turned = jnp.einsum("kpij,dj->kpid", own_block, order, precision=lax.Precision.HIGHEST)
    return jnp.einsum("bi,kpid->kpbd", order, turned, precision=lax.Precision.HIGHEST)


def solution(mesh):
    placed = (P("snap", "cell"), P(), P())
    return jax.shard_map(
        on_device,
        mesh=mesh,
        in_specs=placed,
        out_specs=P("snap", None, None, None),
        check_vma=False,
    )
```
